256 devices in a mesh: slab: 4 (over z_hi, core), row: 64 (over z_lo, x, y).
Axes of the slice: x: 4, y: 4, z: 8 (z_hi: 2, z_lo: 4; z = z_hi * 4 + z_lo), core: 2. Of those that a mesh axis runs over, the one named last changes fastest.
Arguments:
- rhs: bfloat16 [3, 2, 64, 8192], P(None, None, None, 'row'), may hold values from -6 to 6
- operator: bfloat16 [4, 2, 8192, 8192], P('slab', None, 'row'), may hold values from -0.046875 to 0.046875
- sources: bfloat16 [4, 3, 2, 64, 8192], P('slab', None, None, None, 'row'), may hold values from -6 to 6
- skeleton: int32 [4, 8192], P('slab'), may hold values from 0 to 8191, each once within a row
Outputs:
- outgoing: bfloat16 [4, 3, 2, 64, 8192], P('slab', None, None, None, 'row')
The draws below stay inside these ranges and needn't reach their ends.
Inputs may be any that keep to these rules, and one draw needn't show every extreme that they name: Each row of skeleton is a permutation of 0 to 8191.
All inputs are finite; a program needn't handle non-finite values.
Results may differ from the reference program's by a relative error of at most 0.0055.
Values may be sent and summed in bfloat16 or wider, within the bound.
No kernel may reach another device: no remote copies, remote signals or barrier semaphores. Data moves between devices by JAX's collectives and lax.ppermute only.
A program may use at most 64 MiB of HBM per device.

```python
import jax
import jax.numpy as jnp
from jax import lax

NI = 8192
B = 64
NB = 3
S = 4
N_SLAB = 4


def block_scale(key, shape, cuts, smallest, high):
    level, own = 1.0, jax.random.fold_in(key, 6)
    for axis_at, parts in cuts:
        heights = jnp.exp(jax.random.uniform(jax.random.fold_in(own, axis_at), (parts,), jnp.float32, smallest / len(cuts), high / len(cuts)))
        level = level * jnp.repeat(heights, shape[axis_at] // parts).reshape([-1 if axis == axis_at else 1 for axis in range(len(shape))])
    return level


def centred(stream_key, shape, scale, limit, shards=(), kind=jnp.bfloat16):
    gain = block_scale(stream_key, shape, shards, -0.22, 0.18) if shards else 1.0
    array = jax.random.normal(stream_key, shape, jnp.float32) * scale * gain
    return jnp.minimum(jnp.maximum(array, -limit), limit).astype(kind)


def setup_inputs(seed: int = 0) -> dict:
    seeds = jax.random.split(jax.random.key(seed), 5)
    rhs = centred(seeds[0], (NB, 2, B, NI), 1.0, 6.0, ((3, 64),))
    operator = centred(seeds[1], (S, 2, NI, NI), (2 * NI) ** -0.5, 0.046875, ((0, 4), (2, 64)))
    sources = centred(seeds[2], (S, NB, 2, B, NI), 1.0, 6.0, ((0, 4), (4, 64)))
    skeleton = jax.vmap(lambda own: jax.random.permutation(own, NI))(jax.random.split(seeds[3], S)).reshape((S, NI)).astype(jnp.int32)
    return {"rhs": rhs, "operator": operator, "sources": sources, "skeleton": skeleton}


def complex_apply(inputs, matrix):
    count = inputs.shape[0]
    width = inputs.shape[2]
    depth = inputs.shape[3]
    rows = matrix.shape[1]
    flat = inputs.reshape(count * 2 * width, depth)
    mflat = matrix.reshape(2 * rows, depth)
    joined = lax.dot_general(flat, mflat, (((1,), (1,)), ((), ())), preferred_element_type=jnp.float32)
    joined = joined.reshape(count, 2, width, 2, rows)
    real_part = joined[:, 0, :, 0] - joined[:, 1, :, 1]
    imag_part = joined[:, 1, :, 0] + joined[:, 0, :, 1]
    return jnp.stack([real_part, imag_part], axis=1)


def reference(rhs, operator, sources, skeleton):
    incoming = rhs
    results = []
    for section in range(N_SLAB):
        ordered = jnp.take(incoming, skeleton[section].astype(jnp.int32), axis=3)
        value = complex_apply(ordered, operator[section]) + sources[section].astype(jnp.float32)
        value = value.astype(jnp.bfloat16)
        results.append(value)
        incoming = value
    return jnp.stack(results)
```

```python
import functools

import jax
import jax.numpy as jnp
from jax import lax
from jax.experimental import pallas as pl
from jax.experimental.pallas import tpu as pltpu
from jax.sharding import PartitionSpec as P


AXES = ("slab", "row")
LANES = 128


def along(parity, v):
    high, gray = v >> 1, (v ^ (v >> 1)) & 1
    return (high, gray) if parity == 0 else (gray, high)


def inverse_along(parity, group, member):
    return next(v for v in range(4) if along(parity, v) == (group, member))


def place(parity, row):
    z, x, y = row >> 4, row >> 2 & 3, row & 3
    (gx, mx), (gy, my) = along(parity, x), along(parity, y)
    return z << 2 | gx << 1 | gy, mx << 1 | my


def row_of(parity, group, member):
    z = group >> 2
    x = inverse_along(parity, group >> 1 & 1, member >> 1)
    y = inverse_along(parity, group & 1, member & 1)
    return z << 4 | x << 2 | y


def exchange(value, target):
    pairs = []
    for source in range(256):
        half, core, row = source >> 7, source >> 6 & 1, source & 63
        half, core, row = target(half, core, row)
        pairs.append((source, half << 7 | core << 6 | row))
    return lax.ppermute(value, AXES, pairs)


def to_group(parity, mask):
    def target(half, core, row):
        group, member = place(parity, row)
        return half, core, row_of(parity, group ^ mask, member)

    return target


def to_member(parity, mask):
    def target(half, core, row):
        of = core if parity is None else parity
        group, member = place(of, row)
        return half, core, row_of(of, group, member ^ mask)

    return target


def other_core(half, core, row):
    return half, core ^ 1, row


def other_half(half, core, row):
    return half ^ 1, core, row ^ 2 << 4


def reorder_kernel(slot_ref, m_ref, *refs):
    outs, turned, placed = refs[:4], refs[4], refs[5]
    blocks = m_ref.shape[2] // LANES

    def turn(block):
        start = pl.multiple_of(block * LANES, LANES)
        for part in range(2):
            tile = m_ref[part, :, pl.ds(start, LANES)].astype(jnp.float32)
            turned[block & 1, :, part, :] = tile.T

    turn(0)

    def body(block, carry):
        @pl.when(block + 1 < blocks)
        def _():
            turn(block + 1)

        for r in range(LANES):
            placed[slot_ref[block * LANES + r]] = turned[block & 1, r]
        return carry

    lax.fori_loop(0, blocks, body, 0)
    rows = outs[0].shape[0]
    step = 256
    for at, out in enumerate(outs):

        def convert(n, carry, at=at, out=out):
            start = pl.multiple_of(n * step, step)
            for part in range(2):
                out[pl.ds(start, step), part * LANES : (part + 1) * LANES] = placed[
                    pl.ds(at * rows + start, step), part, :
                ].astype(out.dtype)
            return carry

        lax.fori_loop(0, rows // step, convert, 0)


def reorder(slots, matrix):
    columns = matrix.shape[2]
    vmem = pl.BlockSpec(memory_space=pltpu.VMEM)
    return pl.pallas_call(
        reorder_kernel,
        out_shape=[jax.ShapeDtypeStruct((columns // 4, 2 * LANES), jnp.bfloat16)] * 4,
        in_specs=[pl.BlockSpec(memory_space=pltpu.SMEM), vmem],
        out_specs=[vmem] * 4,
        scratch_shapes=[
            pltpu.VMEM((2, LANES, 2, LANES), jnp.float32),
            pltpu.VMEM((columns, 2, LANES), jnp.float32),
        ],
        cost_estimate=pl.CostEstimate(
            flops=0, bytes_accessed=60 * 1024 * 1024, transcendentals=0
        ),
        name="reorder",
    )(slots, matrix)


def product_kernel(own_ref, x0, x1, x2, x3, *refs):
    own, other, outs = refs[:4], refs[4:8], refs[8:12]
    weights, joined, sems = refs[12:]
    use_own = own_ref[0] == 1

    for source, wanted in ((own, use_own), (other, jnp.logical_not(use_own))):

        @pl.when(wanted)
        def _(source=source):
            for m in range(4):
                pltpu.make_async_copy(source[m], weights.at[m], sems.at[m]).start()

    width = joined.shape[0]
    for at, piece in enumerate((x0, x1, x2, x3)):
        for z in range(4):
            start = (z * 4 + at) * LANES
            joined[:, start : start + LANES] = piece[z * width : (z + 1) * width]
    half = width // 6
    for m in range(4):
        pltpu.make_async_copy(own[m], weights.at[m], sems.at[m]).wait()
        both = jnp.dot(joined[...], weights[m], preferred_element_type=jnp.float32)
        both = both.reshape(3, 2, half, 2 * LANES)
        outs[m][:, 0] = both[:, 0, :, :LANES] - both[:, 1, :, LANES:]
        outs[m][:, 1] = both[:, 1, :, :LANES] + both[:, 0, :, LANES:]


def product(use_own, pieces, own, other):
    depth = own[0].shape[0]
    width = pieces[0].shape[0] // 4
    vmem = pl.BlockSpec(memory_space=pltpu.VMEM)
    anywhere = pl.BlockSpec(memory_space=pl.ANY)
    return pl.pallas_call(
        product_kernel,
        out_shape=[jax.ShapeDtypeStruct((3, 2, width // 6, LANES), jnp.float32)] * 4,
        in_specs=[pl.BlockSpec(memory_space=pltpu.SMEM)] + [vmem] * 4 + [anywhere] * 8,
        out_specs=[vmem] * 4,
        scratch_shapes=[
            pltpu.VMEM((4, depth, 2 * LANES), jnp.bfloat16),
            pltpu.VMEM((width, depth), jnp.bfloat16),
            pltpu.SemaphoreType.DMA((4,)),
        ],
        name="product",
    )(use_own, *pieces, *own, *other)


def gather(parity, value):
    flat = value.reshape(-1, LANES)
    parts = [flat] + [exchange(flat, to_group(parity, z << 2)) for z in (1, 2, 3)]
    joined = jnp.concatenate(parts, axis=0)
    return [joined] + [exchange(joined, to_group(parity, at)) for at in (1, 2, 3)]


def on_device(rhs, operator, sources, skeleton):
    slab, row = lax.axis_index("slab"), lax.axis_index("row")
    half, core = slab >> 1, slab & 1
    share = rhs.shape[2] // 2

    def placed(r):
        (g0, m0), (g1, m1) = place(0, r), place(1, r)
        return jnp.where(core == 0, g0, g1), jnp.where(core == 0, m0, m1)

    source = skeleton[0]
    from_row = source >> 7
    from_row = from_row ^ jnp.where(slab == 2, 2 << 4, 0)
    group, member = placed(from_row)
    my_group, my_member = placed(row)
    slots = (member ^ my_member) << 11 | (group ^ my_group) << 7 | source & 127

    mine = lax.dynamic_slice_in_dim(rhs, core * share, share, 2)
    pieces = gather(0, mine)

    added_mine = lax.dynamic_slice_in_dim(sources[0], core * share, share, 2)
    added_sent = lax.dynamic_slice_in_dim(sources[0], (1 - core) * share, share, 2)
    added_other = exchange(added_sent, other_core)

    sent = reorder(slots, operator[0])
    own = [sent[0]] + [exchange(sent[m], to_member(None, m)) for m in (1, 2, 3)]
    other = [exchange(block, other_core) for block in own]

    values = []
    for step in range(4):
        parity = step & 1
        use_own = (core == parity).astype(jnp.int32).reshape(1)
        if step == 2:
            value = exchange(value, other_half)
        if step:
            pieces = gather(parity, value)
        partial = product(use_own, pieces, own, other)
        total = partial[0]
        for m in (1, 2, 3):
            total = total + exchange(partial[m], to_member(parity, m))
        added = jnp.where(core == parity, added_mine, added_other)
        value = (total + added.astype(jnp.float32)).astype(jnp.bfloat16)
        values.append(value)
    first = jnp.where(half == 0, values[0], values[2])
    second = jnp.where(half == 0, values[1], values[3])
    kept = jnp.where(core == 0, first, second)
    arrived = exchange(jnp.where(core == 0, second, first), other_core)
    low = jnp.where(core == 0, kept, arrived)
    high = jnp.where(core == 0, arrived, kept)
    return jnp.concatenate([low, high], axis=2)[None]


def solution(mesh):
    return jax.shard_map(
        on_device,
        mesh=mesh,
        in_specs=(
            P(None, None, None, "row"),
            P("slab", None, "row", None),
            P("slab", None, None, None, "row"),
            P("slab", None),
        ),
        out_specs=P("slab", None, None, None, "row"),
        check_vma=False,
    )
```

```python
import jax
import jax.numpy as jnp
from jax import lax
from jax.experimental import pallas as pl
from jax.experimental.pallas import tpu as pltpu
from jax.sharding import PartitionSpec as P


AXES = ("slab", "row")
LANES = 128


def along(parity, v):
    high, gray = v >> 1, (v ^ (v >> 1)) & 1
    return (high, gray) if parity == 0 else (gray, high)


def inverse_along(parity, group, member):
    return next(v for v in range(4) if along(parity, v) == (group, member))


def place(parity, row):
    z, x, y = row >> 4, row >> 2 & 3, row & 3
    (gx, mx), (gy, my) = along(parity, x), along(parity, y)
    return z << 2 | gx << 1 | gy, mx << 1 | my


def row_of(parity, group, member):
    z = group >> 2
    x = inverse_along(parity, group >> 1 & 1, member >> 1)
    y = inverse_along(parity, group & 1, member & 1)
    return z << 4 | x << 2 | y


def exchange(value, target):
    pairs = []
    for source in range(256):
        half, core, row = source >> 7, source >> 6 & 1, source & 63
        half, core, row = target(half, core, row)
        pairs.append((source, half << 7 | core << 6 | row))
    return lax.ppermute(value, AXES, pairs)


def to_group(parity, mask):
    def target(half, core, row):
        group, member = place(parity, row)
        return half, core, row_of(parity, group ^ mask, member)

    return target


def to_member(parity, mask):
    def target(half, core, row):
        of = core if parity is None else parity
        group, member = place(of, row)
        return half, core, row_of(of, group, member ^ mask)

    return target


def other_core(half, core, row):
    return half, core ^ 1, row


def other_half(half, core, row):
    return half ^ 1, core, row ^ 2 << 4


def reorder_kernel(slot_ref, m_ref, *refs):
    outs, turned, placed = refs[:4], refs[4:6], refs[6]
    blocks = m_ref.shape[2] // LANES

    def turn(block, at):
        start = pl.multiple_of(block * LANES, LANES)
        for part in range(2):
            tile = m_ref[part, :, pl.ds(start, LANES)].astype(jnp.float32)
            turned[at][pl.ds(part, LANES, stride=2), :] = tile.T

    def put(block, at):
        slots = slot_ref.at[pl.ds(pl.multiple_of(block * LANES, LANES), LANES)]
        for r in range(LANES):
            to = pl.multiple_of(slots[r], 2)
            placed[pl.ds(to, 2), :] = turned[at][2 * r : 2 * r + 2, :]

    turn(0, 0)

    def body(pair, carry):
        turn(2 * pair + 1, 1)
        put(2 * pair, 0)
        turn(jnp.minimum(2 * pair + 2, blocks - 1), 0)
        put(2 * pair + 1, 1)
        return carry

    lax.fori_loop(0, blocks // 2, body, 0)
    rows = outs[0].shape[0]
    step = 256
    for at, out in enumerate(outs):

        def convert(n, carry, at=at, out=out):
            start = pl.multiple_of(n * step, step)
            base = 2 * (at * rows + start)
            for part in range(2):
                out[pl.ds(start, step), part * LANES : (part + 1) * LANES] = placed[
                    pl.ds(base + part, step, stride=2), :
                ].astype(out.dtype)
            return carry

        lax.fori_loop(0, rows // step, convert, 0)


def reorder(slots, matrix):
    columns = matrix.shape[2]
    vmem = pl.BlockSpec(memory_space=pltpu.VMEM)
    return pl.pallas_call(
        reorder_kernel,
        out_shape=[jax.ShapeDtypeStruct((columns // 4, 2 * LANES), jnp.bfloat16)] * 4,
        in_specs=[pl.BlockSpec(memory_space=pltpu.SMEM), vmem],
        out_specs=[vmem] * 4,
        scratch_shapes=[
            pltpu.VMEM((2 * LANES, LANES), jnp.float32),
            pltpu.VMEM((2 * LANES, LANES), jnp.float32),
            pltpu.VMEM((2 * columns, LANES), jnp.float32),
        ],
        cost_estimate=pl.CostEstimate(
            flops=0, bytes_accessed=40 * 1024 * 1024, transcendentals=0
        ),
        name="reorder",
    )(slots, matrix)


def product_kernel(own_ref, x0, x1, x2, x3, *refs):
    own, other, outs, joined = refs[:4], refs[4:8], refs[8:12], refs[12]
    use_own = own_ref[0] == 1
    width = joined.shape[0]
    for at, piece in enumerate((x0, x1, x2, x3)):
        for z in range(4):
            start = (z * 4 + at) * LANES
            joined[:, start : start + LANES] = piece[z * width : (z + 1) * width]
    half = width // 6

    for weights, wanted in ((own, use_own), (other, jnp.logical_not(use_own))):

        @pl.when(wanted)
        def _(weights=weights):
            for m in range(4):
                both = jnp.dot(
                    joined[...], weights[m][...], preferred_element_type=jnp.float32
                )
                both = both.reshape(3, 2, half, 2 * LANES)
                outs[m][:, 0] = both[:, 0, :, :LANES] - both[:, 1, :, LANES:]
                outs[m][:, 1] = both[:, 1, :, :LANES] + both[:, 0, :, LANES:]


def product(use_own, pieces, own, other):
    depth = own[0].shape[0]
    width = pieces[0].shape[0] // 4
    vmem = pl.BlockSpec(memory_space=pltpu.VMEM)
    return pl.pallas_call(
        product_kernel,
        out_shape=[jax.ShapeDtypeStruct((3, 2, width // 6, LANES), jnp.float32)] * 4,
        in_specs=[pl.BlockSpec(memory_space=pltpu.SMEM)] + [vmem] * 12,
        out_specs=[vmem] * 4,
        scratch_shapes=[pltpu.VMEM((width, depth), jnp.bfloat16)],
        compiler_params=pltpu.CompilerParams(vmem_limit_bytes=24 * 1024 * 1024),
        name="product",
    )(use_own, *pieces, *own, *other)


def gather(step, value):
    parity = step & 1
    flat = value.reshape(-1, LANES)
    parts = [flat] + [exchange(flat, to_group(parity, z << 2)) for z in (1, 2, 3)]
    joined = jnp.concatenate(parts, axis=0)
    return [joined] + [exchange(joined, to_group(parity, at)) for at in (1, 2, 3)]


def sweep(rhs, operator, sources, skeleton):
    slab, row = lax.axis_index("slab"), lax.axis_index("row")
    half, core = slab >> 1, slab & 1
    share = rhs.shape[2] // 2

    def placed(r):
        (g0, m0), (g1, m1) = place(0, r), place(1, r)
        return jnp.where(core == 0, g0, g1), jnp.where(core == 0, m0, m1)

    source = skeleton[0]
    from_row = source >> 7
    from_row = from_row ^ jnp.where(slab == 2, 2 << 4, 0)
    group, member = placed(from_row)
    my_group, my_member = placed(row)
    slots = (member ^ my_member) << 12 | (group ^ my_group) << 8 | (source & 127) << 1

    mine = lax.dynamic_slice_in_dim(rhs, core * share, share, 2)
    pieces = gather(0, mine)

    added_mine = lax.dynamic_slice_in_dim(sources[0], core * share, share, 2)
    added_sent = lax.dynamic_slice_in_dim(sources[0], (1 - core) * share, share, 2)
    added_other = exchange(added_sent, other_core)

    sent = reorder(slots, operator[0])
    own = [sent[0]] + [exchange(sent[m], to_member(None, m)) for m in (1, 2, 3)]
    other = [exchange(block, other_core) for block in own]

    values = []
    for step in range(4):
        parity = step & 1
        use_own = (core == parity).astype(jnp.int32).reshape(1)
        if step == 2:
            value = exchange(value, other_half)
        if step:
            pieces = gather(step, value)
        partial = product(use_own, pieces, own, other)
        total = partial[0]
        for m in (1, 2, 3):
            total = total + exchange(partial[m], to_member(parity, m))
        added = jnp.where(core == parity, added_mine, added_other)
        value = (total + added.astype(jnp.float32)).astype(jnp.bfloat16)
        values.append(value)
    first = jnp.where(half == 0, values[0], values[2])
    second = jnp.where(half == 0, values[1], values[3])
    kept = jnp.where(core == 0, first, second)
    arrived = exchange(jnp.where(core == 0, second, first), other_core)
    low = jnp.where(core == 0, kept, arrived)
    high = jnp.where(core == 0, arrived, kept)
    return jnp.concatenate([low, high], axis=2)[None]


def solution(mesh):
    return jax.shard_map(
        sweep,
        mesh=mesh,
        in_specs=(
            P(None, None, None, "row"),
            P("slab", None, "row", None),
            P("slab", None, None, None, "row"),
            P("slab", None),
        ),
        out_specs=P("slab", None, None, None, "row"),
        check_vma=False,
    )
```

```python
import functools

import jax
import jax.numpy as jnp
from jax import lax
from jax.experimental import pallas as pl
from jax.experimental.pallas import tpu as pltpu
from jax.sharding import PartitionSpec as P


AXES = ("slab", "row")
LANES = 128


def along(parity, v):
    high, gray = v >> 1, (v ^ (v >> 1)) & 1
    return (high, gray) if parity == 0 else (gray, high)


def inverse_along(parity, group, member):
    return next(v for v in range(4) if along(parity, v) == (group, member))


def place(parity, row):
    z, x, y = row >> 4, row >> 2 & 3, row & 3
    (gx, mx), (gy, my) = along(parity, x), along(parity, y)
    return z << 2 | gx << 1 | gy, mx << 1 | my


def row_of(parity, group, member):
    z = group >> 2
    x = inverse_along(parity, group >> 1 & 1, member >> 1)
    y = inverse_along(parity, group & 1, member & 1)
    return z << 4 | x << 2 | y


def exchange(value, target):
    pairs = []
    for source in range(256):
        half, core, row = source >> 7, source >> 6 & 1, source & 63
        half, core, row = target(half, core, row)
        pairs.append((source, half << 7 | core << 6 | row))
    return lax.ppermute(value, AXES, pairs)


def to_group(parity, mask):
    def target(half, core, row):
        group, member = place(parity, row)
        return half, core, row_of(parity, group ^ mask, member)

    return target


def to_member(parity, mask):
    def target(half, core, row):
        of = core if parity is None else parity
        group, member = place(of, row)
        return half, core, row_of(of, group, member ^ mask)

    return target


def other_core(half, core, row):
    return half, core ^ 1, row


def other_half(half, core, row):
    return half ^ 1, core, row ^ 2 << 4


def reorder_kernel(slot_ref, m_ref, *refs):
    outs, turned, placed = refs[:4], refs[4:6], refs[6]
    blocks = m_ref.shape[2] // LANES

    def turn(block, at):
        start = pl.multiple_of(block * LANES, LANES)
        for part in range(2):
            tile = m_ref[part, :, pl.ds(start, LANES)].astype(jnp.float32)
            turned[at][pl.ds(part, LANES, stride=2), :] = tile.T

    def put(block, at):
        slots = slot_ref.at[pl.ds(pl.multiple_of(block * LANES, LANES), LANES)]
        for r in range(LANES):
            to = pl.multiple_of(slots[r], 2)
            placed[pl.ds(to, 2), :] = turned[at][2 * r : 2 * r + 2, :]

    turn(0, 0)

    def body(pair, carry):
        turn(2 * pair + 1, 1)
        put(2 * pair, 0)
        turn(jnp.minimum(2 * pair + 2, blocks - 1), 0)
        put(2 * pair + 1, 1)
        return carry

    lax.fori_loop(0, blocks // 2, body, 0)
    rows = outs[0].shape[0]
    step = 256
    for at, out in enumerate(outs):

        def convert(n, carry, at=at, out=out):
            start = pl.multiple_of(n * step, step)
            base = 2 * (at * rows + start)
            for part in range(2):
                out[pl.ds(start, step), part * LANES : (part + 1) * LANES] = placed[
                    pl.ds(base + part, step, stride=2), :
                ].astype(out.dtype)
            return carry

        lax.fori_loop(0, rows // step, convert, 0)


def reorder(slots, matrix):
    columns = matrix.shape[2]
    vmem = pl.BlockSpec(memory_space=pltpu.VMEM)
    return pl.pallas_call(
        reorder_kernel,
        out_shape=[jax.ShapeDtypeStruct((columns // 4, 2 * LANES), jnp.bfloat16)] * 4,
        in_specs=[pl.BlockSpec(memory_space=pltpu.SMEM), vmem],
        out_specs=[vmem] * 4,
        scratch_shapes=[
            pltpu.VMEM((2 * LANES, LANES), jnp.float32),
            pltpu.VMEM((2 * LANES, LANES), jnp.float32),
            pltpu.VMEM((2 * columns, LANES), jnp.float32),
        ],
        cost_estimate=pl.CostEstimate(
            flops=0, bytes_accessed=40 * 1024 * 1024, transcendentals=0
        ),
        compiler_params=pltpu.CompilerParams(vmem_limit_bytes=24 * 1024 * 1024),
        name="reorder",
    )(slots, matrix)


def product_kernel(outer, own_ref, x0, x1, x2, x3, *refs):
    own, other, outs, joined = refs[:4], refs[4:8], refs[8:12], refs[12]
    use_own = own_ref[0] == 1
    width = joined.shape[0]
    for at, piece in enumerate((x0, x1, x2, x3)):
        for n in range(4):
            start = (at * outer + n * (4 // outer)) * LANES
            joined[:, start : start + LANES] = piece[n * width : (n + 1) * width]
    half = width // 6

    for weights, wanted in ((own, use_own), (other, jnp.logical_not(use_own))):

        @pl.when(wanted)
        def _(weights=weights):
            for m in range(4):
                both = jnp.dot(
                    joined[...], weights[m][...], preferred_element_type=jnp.float32
                )
                both = both.reshape(3, 2, half, 2 * LANES)
                outs[m][:, 0] = both[:, 0, :, :LANES] - both[:, 1, :, LANES:]
                outs[m][:, 1] = both[:, 1, :, :LANES] + both[:, 0, :, LANES:]


def product(step, use_own, pieces, own, other):
    depth = own[0].shape[0]
    width = pieces[0].shape[0] // 4
    vmem = pl.BlockSpec(memory_space=pltpu.VMEM)
    return pl.pallas_call(
        functools.partial(product_kernel, 4 if step == 0 else 1),
        out_shape=[jax.ShapeDtypeStruct((3, 2, width // 6, LANES), jnp.float32)] * 4,
        in_specs=[pl.BlockSpec(memory_space=pltpu.SMEM)] + [vmem] * 12,
        out_specs=[vmem] * 4,
        scratch_shapes=[pltpu.VMEM((width, depth), jnp.bfloat16)],
        compiler_params=pltpu.CompilerParams(vmem_limit_bytes=12 * 1024 * 1024),
        name="product",
    )(use_own, *pieces, *own, *other)


def gather(step, value):
    parity = step & 1
    flat = value.reshape(-1, LANES)
    inner, outer = (1, 4) if step == 0 else (4, 1)
    parts = [flat] + [exchange(flat, to_group(parity, n * inner)) for n in (1, 2, 3)]
    joined = jnp.concatenate(parts, axis=0)
    return [joined] + [exchange(joined, to_group(parity, n * outer)) for n in (1, 2, 3)]


def sweep(rhs, operator, sources, skeleton):
    slab, row = lax.axis_index("slab"), lax.axis_index("row")
    half, core = slab >> 1, slab & 1
    share = rhs.shape[2] // 2

    def placed(r):
        (g0, m0), (g1, m1) = place(0, r), place(1, r)
        return jnp.where(core == 0, g0, g1), jnp.where(core == 0, m0, m1)

    source = skeleton[0]
    from_row = source >> 7
    from_row = from_row ^ jnp.where(slab == 2, 2 << 4, 0)
    group, member = placed(from_row)
    my_group, my_member = placed(row)
    slots = (member ^ my_member) << 12 | (group ^ my_group) << 8 | (source & 127) << 1

    mine = lax.dynamic_slice_in_dim(rhs, core * share, share, 2)
    pieces = gather(0, mine)

    added_mine = lax.dynamic_slice_in_dim(sources[0], core * share, share, 2)
    added_sent = lax.dynamic_slice_in_dim(sources[0], (1 - core) * share, share, 2)
    added_other = exchange(added_sent, other_core)

    sent = reorder(slots, operator[0])
    own = [sent[0]] + [exchange(sent[m], to_member(None, m)) for m in (1, 2, 3)]
    other = [exchange(block, other_core) for block in own]

    values = []
    for step in range(4):
        parity = step & 1
        use_own = (core == parity).astype(jnp.int32).reshape(1)
        if step == 2:
            value = exchange(value, other_half)
        if step:
            pieces = gather(step, value)
        partial = product(step, use_own, pieces, own, other)
        total = partial[0]
        for m in (1, 2, 3):
            total = total + exchange(partial[m], to_member(parity, m))
        added = jnp.where(core == parity, added_mine, added_other)
        value = (total + added.astype(jnp.float32)).astype(jnp.bfloat16)
        values.append(value)
    first = jnp.where(half == 0, values[0], values[2])
    second = jnp.where(half == 0, values[1], values[3])
    kept = jnp.where(core == 0, first, second)
    arrived = exchange(jnp.where(core == 0, second, first), other_core)
    low = jnp.where(core == 0, kept, arrived)
    high = jnp.where(core == 0, arrived, kept)
    return jnp.concatenate([low, high], axis=2)[None]


def solution(mesh):
    return jax.shard_map(
        sweep,
        mesh=mesh,
        in_specs=(
            P(None, None, None, "row"),
            P("slab", None, "row", None),
            P("slab", None, None, None, "row"),
            P("slab", None),
        ),
        out_specs=P("slab", None, None, None, "row"),
        check_vma=False,
    )
```
